128 devices in a mesh: tm: 16 (over z, x), space: 8 (over y, core).
Axes of the slice: x: 4, y: 4, z: 4, core: 2. Of those that a mesh axis runs over, the one named last changes fastest.
Arguments:
- ensembles: bfloat16 [256, 80, 16384], P('tm', None, 'space'), may hold values from -6 to 6
- cotangents: bfloat16 [256, 80, 16384], P('tm', None, 'space'), may hold values from -6 to 6
- transforms: float32 [256, 80, 80], P('tm'), may hold values from -1.5 to 1.5
Outputs:
- smoothed: bfloat16 [256, 80, 16384], P('tm', None, 'space')
- ensemble_grad: bfloat16 [256, 80, 16384], P('tm', None, 'space')
- transform_grad: float32 [256, 80, 80], P('tm')
The draws below stay inside these ranges and needn't reach their ends.
All inputs are finite; a program needn't handle non-finite values.
Results may differ from the reference program's by a relative error of at most 0.0049.
Values sent between devices are 32-bit elements; how exact they have to be, the bound alone decides.
A program may use at most 64 MiB of HBM per device.

```python
import jax
import jax.numpy as jnp
from jax import lax

MEMBERS = 80
TIMES = 256
CELLS = 16384


def draw_transforms(key, part):
    first_key, second_key = jax.random.split(jax.random.fold_in(key, 11))
    noise = jax.random.normal(first_key, (TIMES, MEMBERS, MEMBERS), jnp.float32)
    gains = jnp.exp(0.05 * jnp.clip(jax.random.normal(second_key, (TIMES, MEMBERS, 1), jnp.float32), -3.0, 3.0))
    skewed = (noise - jnp.swapaxes(noise, 1, 2)) * (0.4 / jnp.sqrt(2.0 * MEMBERS))
    squared = jnp.einsum('tij,tjk->tik', skewed, skewed, precision=lax.Precision.HIGHEST)
    rotation = jnp.eye(MEMBERS, dtype=jnp.float32)[None] + skewed + 0.5 * squared
    return (rotation * gains).astype(jnp.float32)


def level_of(stream_key, shape, pieces, low, largest):
    gain = 1.0
    for axis_at, parts in pieces:
        draws = jax.random.uniform(jax.random.fold_in(jax.random.fold_in(stream_key, 6), axis_at), (parts,), jnp.float32, low / len(pieces), largest / len(pieces))
        gain = gain * jnp.repeat(jnp.exp(draws), shape[axis_at] // parts).reshape((-1,) + (1,) * (len(shape) - 1 - axis_at))
    return gain


def scatter_about(rng, dims, width, limit, pieces=(), kind=jnp.bfloat16):
    loudness = level_of(rng, dims, pieces, -0.22, 0.18) if pieces else 1.0
    result = jax.random.normal(rng, dims, jnp.float32) * width * loudness
    return jnp.minimum(jnp.maximum(result, -limit), limit).astype(kind)


def setup_inputs(seed: int = 0) -> dict:
    key_of = jax.random.split(jax.random.key(seed), 4)
    ensembles = scatter_about(key_of[0], (TIMES, MEMBERS, CELLS), 1.0, 6.0, ((0, 16), (2, 8)))
    cotangents = scatter_about(key_of[1], (TIMES, MEMBERS, CELLS), 1.0, 6.0, ((0, 16), (2, 8)))
    transforms = draw_transforms(jax.random.fold_in(key_of[3], 71), 0)
    return {"ensembles": ensembles, "cotangents": cotangents, "transforms": transforms}


def reference(ensembles, cotangents, transforms):
    exact_mode = lax.Precision.HIGHEST
    identity = jnp.eye(MEMBERS, dtype=jnp.float32)

    def backward(following_prod, weight):
        current = jnp.dot(weight, following_prod, precision=exact_mode)
        return (current, (current, following_prod))
    _, (products, following) = lax.scan(backward, identity, transforms, reverse=True)
    rounded = products.astype(jnp.bfloat16)

    def smooth_one(index):
        block = ensembles[index].astype(jnp.float32)
        weights = cotangents[index].astype(jnp.float32)
        factor = rounded[index].astype(jnp.float32)
        smoothed_one = jnp.dot(factor.T, block, precision=exact_mode).astype(jnp.bfloat16)
        grad_one = jnp.dot(factor, weights, precision=exact_mode).astype(jnp.bfloat16)
        gram_one = jnp.dot(block, weights.T, precision=exact_mode)
        return (smoothed_one, grad_one, gram_one)
    smoothed, ensemble_grad, gram = lax.map(smooth_one, jnp.arange(TIMES, dtype=jnp.int32))

    def forward(message, inputs):
        weight, gram_one = inputs
        total = gram_one + message
        return (jnp.dot(weight.T, total, precision=exact_mode), total)
    _, totals = lax.scan(forward, jnp.zeros((MEMBERS, MEMBERS), jnp.float32), (transforms, gram))
    scale = 1.0 / jnp.sqrt(jnp.float32(CELLS) * jnp.float32(TIMES))
    transform_grad = jnp.einsum('tkm,tjm->tkj', totals, following, precision=exact_mode) * scale
    return (smoothed, ensemble_grad, transform_grad)
```

```python
import functools
import math

import jax
import jax.numpy as jnp
from jax import lax
from jax.experimental import pallas as pl
from jax.experimental.pallas import tpu as pltpu
from jax.sharding import PartitionSpec as P

MESH = pl.DeviceIdType.MESH
f32 = jnp.float32
bf16 = jnp.bfloat16


def mm(a, b, dims=((1,), (0,))):
    return lax.dot_general(
        a, b, (dims, ((), ())), precision=lax.Precision.HIGHEST, preferred_element_type=f32
    )


def block_scans(tr, count, prefix_ref, suffix_ref):
    groups = count // 4
    heads, tails = [], []
    for g in range(groups):
        w = [tr[4 * g + i] for i in range(4)]
        w01, w23 = mm(w[0], w[1]), mm(w[2], w[3])
        heads.append((w[0], w01, mm(w01, w[2]), mm(w01, w23)))
        tails.append((None, mm(w[1], w23), w23, w[3]))
    before = None
    for g in range(groups):
        for i in range(4):
            if g == 0 and i == 0:
                continue
            if i == 0:
                prefix_ref[4 * g] = before
            elif g == 0:
                prefix_ref[i] = heads[0][i - 1]
            else:
                prefix_ref[4 * g + i] = mm(before, heads[g][i - 1])
        before = heads[g][3] if g == 0 else mm(before, heads[g][3])
    after = None
    for g in reversed(range(groups)):
        whole = heads[g][3]
        parts = (whole,) + tails[g][1:]
        for i in range(4):
            suffix_ref[4 * g + i] = parts[i] if after is None else mm(parts[i], after)
        after = whole if after is None else mm(whole, after)


def block_total(tr, count):
    level = [tr[i] for i in range(count)]
    while len(level) > 1:
        level = [mm(level[i], level[i + 1]) for i in range(0, len(level), 2)]
    return level[0]


def exchange_kernel(
    n_tm, n_sp, times, members,
    e_hbm, c_hbm, t_hbm,
    e_v, c_v, lt_out, pre_out, prod_out, mt_out,
    tr, p_own, p_buf, ltp, lt_rx, lt_core, lt_ry, lt_fin, ot_own, ot_rx, ot_buf, mt_buf, suf,
    in_sem, p_s, p_r, pf_s, pf_r, lp_s, lp_r, ly_s, ly_r, la_s, la_r, lf_s, lf_r,
    or_s, or_r, ot_s, ot_r, mx_s, mx_r,
):
    half = members // 2
    n_y = n_sp // 2
    per_core = times // 2
    own = per_core // n_y
    me = lax.axis_index("tm")
    sp = lax.axis_index("space")
    y = sp // 2
    c = lax.rem(sp, 2)
    partner = 2 * y + (1 - c)

    def tm_peer(d):
        return lax.rem(me + d, n_tm)

    def sp_peer(d):
        return lax.rem(sp + d, n_sp)

    def remote(src, dst, s_sem, r_sem, device):
        return pltpu.make_async_remote_copy(
            src_ref=src, dst_ref=dst, send_sem=s_sem, recv_sem=r_sem,
            device_id=device, device_id_type=MESH,
        )

    t_copy = pltpu.make_async_copy(t_hbm, tr, in_sem.at[2 * times])
    t_copy.start()
    loads = []
    for t in range(times):
        loads.append((
            pltpu.make_async_copy(e_hbm.at[t], e_v.at[t], in_sem.at[t]),
            pltpu.make_async_copy(c_hbm.at[t], c_v.at[t], in_sem.at[times + t]),
        ))
        for copy in loads[-1]:
            copy.start()

    barrier = pltpu.get_barrier_semaphore()
    for d in range(1, n_tm):
        pl.semaphore_signal(barrier, inc=1, device_id={"tm": tm_peer(d)}, device_id_type=MESH)
    for d in range(1, n_sp):
        pl.semaphore_signal(barrier, inc=1, device_id={"space": sp_peer(d)}, device_id_type=MESH)

    t_copy.wait()
    total = block_total(tr, times)
    p_own[0] = total[:half]
    p_own[1] = total[half:]
    p_buf[c, me] = p_own[c]

    pl.semaphore_wait(barrier, n_tm - 1 + n_sp - 1)

    p_copies = []
    for d in range(1, n_tm):
        copy = remote(p_own.at[c], p_buf.at[c, me], p_s.at[d], p_r.at[d], {"tm": tm_peer(d)})
        copy.start()
        p_copies.append(copy)

    lp_copies = []
    waiting = []
    state = None
    for pair in range(times // 2 + 1):
        if pair < times // 2:
            for t in (2 * pair, 2 * pair + 1):
                for copy in loads[t]:
                    copy.wait()
            fresh = [
                lax.dot_general(
                    c_v[t], e_v[t], (((1,), (1,)), ((), ())), preferred_element_type=f32
                )
                for t in (2 * pair, 2 * pair + 1)
            ]
        else:
            fresh = []
        if pair > 0:
            for k, gram in enumerate(waiting):
                t = 2 * (pair - 1) + k
                state = gram if t == 0 else gram + mm(state, tr[t - 1])
                ltp[t] = state
            j = pair - 1
            copy = remote(
                ltp.at[2 * j + 1 - c], lt_rx.at[j], lp_s.at[j], lp_r.at[j], {"space": partner}
            )
            copy.start()
            lp_copies.append(copy)
        waiting = fresh

    leaving = mm(state, tr[times - 1])
    ot_own[0] = leaving[:half]
    ot_own[1] = leaving[half:]
    or_copies = []
    for d in range(1, n_sp):
        peer = sp_peer(d)
        copy = remote(
            ot_own.at[lax.rem(peer, 2)], ot_rx.at[d], or_s.at[d], or_r.at[d], {"space": peer}
        )
        copy.start()
        or_copies.append(copy)

    for j in range(per_core):
        lp_copies[j].wait_recv()
        lt_core[j] = ltp[2 * j + c] + lt_rx[j]
    ly_copies = []
    for d in range(1, n_y):
        q = lax.rem(y + d, n_y)
        copy = remote(
            lt_core.at[pl.ds(q * own, own)], lt_ry.at[d], ly_s.at[d], ly_r.at[d],
            {"space": 2 * q + c},
        )
        copy.start()
        ly_copies.append(copy)

    block_scans(tr, times, pre_out, suf)

    pf_copies = []
    own_copy = remote(
        p_own.at[c], p_buf.at[c, me], pf_s.at[0], pf_r.at[0], {"space": partner}
    )
    own_copy.start()
    pf_copies.append(own_copy)

    summed = ot_own[c]
    for d in range(1, n_sp):
        or_copies[d - 1].wait_recv()
        summed = summed + ot_rx[d]
    ot_buf[me] = summed
    ot_copies = []
    for d in range(1, n_tm):
        copy = remote(ot_buf.at[me], ot_buf.at[me], ot_s.at[d], ot_r.at[d], {"tm": tm_peer(d)})
        copy.start()
        ot_copies.append(copy)

    for d in range(1, n_tm):
        p_copies[d - 1].wait_recv()
        source = lax.rem(me + n_tm - d, n_tm)
        copy = remote(
            p_buf.at[c, source], p_buf.at[c, source], pf_s.at[d], pf_r.at[d], {"space": partner}
        )
        copy.start()
        pf_copies.append(copy)

    mine = [lt_core[y * own + k] for k in range(own)]
    for d in range(1, n_y):
        ly_copies[d - 1].wait_recv()
        mine = [mine[k] + lt_ry[d, k] for k in range(own)]
    for k in range(own):
        lt_fin[c, y, k] = mine[k]
    la_copies = []
    for d in range(1, n_y):
        q = lax.rem(y + d, n_y)
        copy = remote(
            lt_fin.at[c, y], lt_fin.at[c, y], la_s.at[d], la_r.at[d], {"space": 2 * q + c}
        )
        copy.start()
        la_copies.append(copy)
    lf_copies = []
    copy = remote(lt_fin.at[c, y], lt_fin.at[c, y], lf_s.at[0], lf_r.at[0], {"space": partner})
    copy.start()
    lf_copies.append(copy)

    for copy in pf_copies:
        copy.wait_recv()

    rows = lax.broadcasted_iota(jnp.int32, (members, members), 0)
    cols = lax.broadcasted_iota(jnp.int32, (members, members), 1)
    later = jnp.where(rows == cols, 1.0, 0.0).astype(f32)
    for b in reversed(range(1, n_tm)):
        whole = jnp.concatenate([p_buf[0, b], p_buf[1, b]], axis=0)
        later = jnp.where(b > me, mm(whole, later), later)
    for t in range(times):
        prod_out[t] = mm(suf[t], later)
    prod_out[times] = later

    for d in range(1, n_y):
        la_copies[d - 1].wait_recv()
        q = lax.rem(y + n_y - d, n_y)
        copy = remote(lt_fin.at[c, q], lt_fin.at[c, q], lf_s.at[d], lf_r.at[d], {"space": partner})
        copy.start()
        lf_copies.append(copy)

    for copy in ot_copies:
        copy.wait_recv()
    entering = jnp.zeros((half, members), f32)
    for b in range(n_tm - 1):
        whole = jnp.concatenate([p_buf[0, b], p_buf[1, b]], axis=0)
        entering = jnp.where(b < me, mm(entering, whole) + ot_buf[b], entering)
    mt_buf[c] = entering
    mx_copy = remote(mt_buf.at[c], mt_buf.at[c], mx_s.at[0], mx_r.at[0], {"space": partner})
    mx_copy.start()

    for copy in lf_copies:
        copy.wait_recv()
    for k in range(2):
        for q in range(n_y):
            for i in range(own):
                lt_out[2 * (q * own + i) + k] = lt_fin[k, q, i]
    mx_copy.wait_recv()
    mt_out[:half] = mt_buf[0]
    mt_out[half:] = mt_buf[1]

    for copy in (
        p_copies + lp_copies + or_copies + ly_copies + pf_copies
        + ot_copies + la_copies + lf_copies + [mx_copy]
    ):
        copy.wait_send()


def output_kernel(
    times, scale,
    e_v, c_v, lt, pre, prod, mt,
    sm_hbm, eg_hbm, tg_hbm,
    sm, eg, tg, sems, tg_sem,
):
    copies = []
    for t in range(times):
        factor = prod[t].astype(bf16)
        sm[t] = lax.dot_general(
            factor, e_v[t], (((0,), (0,)), ((), ())), preferred_element_type=f32
        ).astype(bf16)
        eg[t] = jnp.dot(factor, c_v[t], preferred_element_type=f32).astype(bf16)
        for k, (src, dst) in enumerate(((sm, sm_hbm), (eg, eg_hbm))):
            copy = pltpu.make_async_copy(src.at[t], dst.at[t], sems.at[k, t])
            copy.start()
            copies.append(copy)
    entering = mt[...]
    for t in range(times):
        total = lt[t] + (entering if t == 0 else mm(entering, pre[t]))
        tg[t] = mm(total, prod[t + 1], ((0,), (1,))) * scale
    copy = pltpu.make_async_copy(tg, tg_hbm, tg_sem)
    copy.start()
    copies.append(copy)
    for copy in copies:
        copy.wait()


def shards(n_tm, n_sp, ensembles, cotangents, transforms):
    times, members, cells = ensembles.shape
    half = members // 2
    n_y = n_sp // 2
    per_core = times // 2
    own = per_core // n_y
    square = (members, members)
    halves = (half, members)
    anywhere = pl.BlockSpec(memory_space=pl.ANY)
    vmem = pl.BlockSpec(memory_space=pltpu.VMEM)
    dma = pltpu.SemaphoreType.DMA
    shape = jax.ShapeDtypeStruct
    big = shape((times, members, cells), bf16)
    stack = shape((times,) + square, f32)
    e_v, c_v, lt, pre, prod, mt = pl.pallas_call(
        functools.partial(exchange_kernel, n_tm, n_sp, times, members),
        out_shape=[big, big, stack, stack, shape((times + 1,) + square, f32), shape(square, f32)],
        in_specs=[pl.BlockSpec(memory_space=pltpu.HBM)] * 3,
        out_specs=[vmem] * 6,
        scratch_shapes=[
            pltpu.VMEM((times,) + square, f32),
            pltpu.VMEM((2,) + halves, f32),
            pltpu.VMEM((2, n_tm) + halves, f32),
            pltpu.VMEM((times,) + square, f32),
            pltpu.VMEM((per_core,) + square, f32),
            pltpu.VMEM((per_core,) + square, f32),
            pltpu.VMEM((n_y, own) + square, f32),
            pltpu.VMEM((2, n_y, own) + square, f32),
            pltpu.VMEM((2,) + halves, f32),
            pltpu.VMEM((n_sp,) + halves, f32),
            pltpu.VMEM((n_tm,) + halves, f32),
            pltpu.VMEM((2,) + halves, f32),
            pltpu.VMEM((times,) + square, f32),
            dma((2 * times + 1,)),
            dma((n_tm,)), dma((n_tm,)),
            dma((n_tm,)), dma((n_tm,)),
            dma((per_core,)), dma((per_core,)),
            dma((n_y,)), dma((n_y,)),
            dma((n_y,)), dma((n_y,)),
            dma((n_y,)), dma((n_y,)),
            dma((n_sp,)), dma((n_sp,)),
            dma((n_tm,)), dma((n_tm,)),
            dma((1,)), dma((1,)),
        ],
        compiler_params=pltpu.CompilerParams(
            collective_id=0, has_side_effects=True, vmem_limit_bytes=24 * 2**20
        ),
        name="exchange",
    )(*(pltpu.with_memory_space_constraint(a, pltpu.HBM) for a in (ensembles, cotangents, transforms)))
    scale = 1.0 / math.sqrt(cells * n_sp * times * n_tm)
    return pl.pallas_call(
        functools.partial(output_kernel, times, scale),
        out_shape=[big, big, stack],
        in_specs=[vmem] * 6,
        out_specs=[anywhere] * 3,
        scratch_shapes=[
            pltpu.VMEM((times, members, cells), bf16),
            pltpu.VMEM((times, members, cells), bf16),
            pltpu.VMEM((times,) + square, f32),
            dma((2, times)),
            dma(()),
        ],
        compiler_params=pltpu.CompilerParams(vmem_limit_bytes=30 * 2**20),
        name="outputs",
    )(e_v, c_v, lt, pre, prod, mt)


def solution(mesh):
    specs = (P("tm", None, "space"), P("tm", None, "space"), P("tm", None, None))
    return jax.shard_map(
        functools.partial(shards, mesh.shape["tm"], mesh.shape["space"]),
        mesh=mesh,
        in_specs=specs,
        out_specs=specs,
        check_vma=False,
    )
```

```python
import functools
import math

import jax
import jax.numpy as jnp
from jax import lax
from jax.experimental import pallas as pl
from jax.experimental.pallas import tpu as pltpu
from jax.sharding import PartitionSpec as P

MESH = pl.DeviceIdType.MESH
PB, PF, OR, OT, OF, LP, LY, LA, LF = range(9)
f32 = jnp.float32
bf16 = jnp.bfloat16


def mm(a, b, dims=((1,), (0,))):
    return lax.dot_general(
        a, b, (dims, ((), ())), precision=lax.Precision.HIGHEST, preferred_element_type=f32
    )


def group_scans(tr, groups):
    heads, tails = [], []
    for g in range(groups):
        w = [tr[4 * g + i] for i in range(4)]
        w01, w23 = mm(w[0], w[1]), mm(w[2], w[3])
        heads.append((w[0], w01, mm(w01, w[2]), mm(w01, w23)))
        tails.append((None, mm(w[1], w23), w23, w[3]))
    return heads, tails


def block_scans(heads, tails, prefix_ref, suffix_ref):
    groups = len(heads)
    before = None
    for g in range(groups):
        for i in range(4):
            if g == 0 and i == 0:
                continue
            if i == 0:
                prefix_ref[4 * g] = before
            elif g == 0:
                prefix_ref[i] = heads[0][i - 1]
            else:
                prefix_ref[4 * g + i] = mm(before, heads[g][i - 1])
        before = heads[g][3] if g == 0 else mm(before, heads[g][3])
    after = None
    for g in reversed(range(groups)):
        whole = heads[g][3]
        parts = (whole,) + tails[g][1:]
        for i in range(4):
            suffix_ref[4 * g + i] = parts[i] if after is None else mm(parts[i], after)
        after = whole if after is None else mm(whole, after)


def block_total(tr, count):
    level = [tr[i] for i in range(count)]
    while len(level) > 1:
        level = [mm(level[i], level[i + 1]) for i in range(0, len(level), 2)]
    return level[0]


def pack(square):
    rows = square.shape[0]
    left, rest, tall = 64, rows - 64, rows // 5
    wide = jnp.concatenate([square[: rows // 2, :left], square[rows // 2 :, :left]], axis=1)
    pieces = [square[tall * g : tall * (g + 1), left:] for g in range(5)]
    pieces.append(jnp.zeros((tall, 2 * left - 5 * rest), f32))
    return jnp.concatenate([wide, jnp.concatenate(pieces, axis=1)], axis=0)


def unpack(packed, rows):
    left, rest, tall = 64, rows - 64, rows // 5
    wide, tail = packed[: rows // 2], packed[rows // 2 :]
    first = jnp.concatenate([wide[:, :left], wide[:, left:]], axis=0)
    last = jnp.concatenate([tail[:, rest * g : rest * (g + 1)] for g in range(5)], axis=0)
    return jnp.concatenate([first, last], axis=1)


def exchange_kernel(
    n_tm, n_sp, times, members,
    e_hbm, c_hbm, t_hbm,
    sm_v, eg_v, lt_out, pre_out, prod_out, p_out, ot_out,
    e_v, c_v, tr, p_own, p_buf, ltp, lt_rx, lt_core, lt_ry, lt_fin, ot_own, ot_rx, ot_buf, suf, scan_buf, gram, carry,
    in_sem, s_sem, r_sem, lp_r, ly_r, la_r, lf_r,
):
    half = members // 2
    n_y = n_sp // 2
    own = times // 2 // n_y
    batch = times // own
    me = lax.axis_index("tm")
    sp = lax.axis_index("space")
    y = sp // 2
    c = lax.rem(sp, 2)
    partner = 2 * y + (1 - c)

    def tm_peer(d):
        return lax.rem(me + d, n_tm)

    def sp_peer(d):
        return lax.rem(sp + d, n_sp)

    def send(src, dst, sems, device):
        pltpu.make_async_remote_copy(
            src_ref=src, dst_ref=dst, send_sem=sems[0], recv_sem=sems[1],
            device_id=device, device_id_type=MESH,
        ).start()

    def wait(ref, sem):
        pltpu.make_async_copy(ref, ref, sem).wait()

    t_copy = pltpu.make_async_copy(t_hbm, tr, in_sem.at[10])
    t_copy.start()
    groups = [(0, 4), (4, 8), (8, 12), (12, 14), (14, 16)]
    loads = []
    for g, (first, last) in enumerate(groups):
        part = pl.ds(first, last - first)
        loads.append((
            pltpu.make_async_copy(e_hbm.at[part], e_v.at[part], in_sem.at[2 * g]),
            pltpu.make_async_copy(c_hbm.at[part], c_v.at[part], in_sem.at[2 * g + 1]),
        ))
        for copy in loads[-1]:
            copy.start()

    barrier = pltpu.get_barrier_semaphore()
    for d in range(1, n_tm):
        pl.semaphore_signal(barrier, inc=1, device_id={"tm": tm_peer(d)}, device_id_type=MESH)
    for d in range(1, n_sp):
        pl.semaphore_signal(barrier, inc=1, device_id={"space": sp_peer(d)}, device_id_type=MESH)

    t_copy.wait()
    total = block_total(tr, times)
    p_own[0] = total[:half]
    p_own[1] = total[half:]
    p_buf[c, me] = p_own[c]

    def send_pairs(first, last):
        k = first // n_y
        part = pl.ds(first, last - first)
        send(ltp.at[1 - c, part], lt_rx.at[part], (s_sem.at[LP], lp_r.at[k]), {"space": partner})

    def reduce_cores(k):
        wait(lt_rx.at[pl.ds(k * n_y, n_y)], lp_r.at[k])
        for j in range(k * n_y, (k + 1) * n_y):
            lt_core[j] = ltp[c, j] + lt_rx[j]
        for d in range(1, n_y):
            q = lax.rem(y + d, n_y)
            send(
                lt_core.at[k * n_y + q], lt_ry.at[k, d - 1], (s_sem.at[LY], ly_r.at[k]),
                {"space": 2 * q + c},
            )

    def hand_round(k):
        wait(lt_ry.at[k], ly_r.at[k])
        mine = lt_core[k * n_y + y]
        for d in range(1, n_y):
            mine = mine + lt_ry[k, d - 1]
        lt_fin[k, c, y] = mine
        for d in range(1, n_y):
            q = lax.rem(y + d, n_y)
            send(
                lt_fin.at[k, c, y], lt_fin.at[k, c, y], (s_sem.at[LA], la_r.at[k]),
                {"space": 2 * q + c},
            )

    def forward_totals(k):
        wait(lt_ry.at[k], la_r.at[k])
        send(lt_fin.at[k, c], lt_fin.at[k, c], (s_sem.at[LF], lf_r.at[k]), {"space": partner})

    before = (0, 0)
    for g, (first, last) in enumerate(groups + [(times, times)]):
        if last > first:
            for copy in loads[g]:
                copy.wait()
        if before[0]:
            state = carry[...]
        for k in range(max(last - first, before[1] - before[0])):
            if first + k < last:
                t = first + k
                gram[t] = lax.dot_general(
                    c_v[t], e_v[t], (((1,), (1,)), ((), ())), preferred_element_type=f32
                )
            if before[0] + k < before[1]:
                t = before[0] + k
                state = gram[t] if t == 0 else gram[t] + mm(state, tr[t - 1])
                ltp[t % 2, t // 2] = pack(state)
        if before[1]:
            carry[...] = state
        if before[1]:
            send_pairs(before[0] // 2, before[1] // 2)
        before = (first, last)
        if g == 0:
            pl.semaphore_wait(barrier, n_tm - 1 + n_sp - 1)
            for d in range(1, n_tm):
                send(p_own.at[c], p_buf.at[c, me], (s_sem.at[PB], r_sem.at[PB]), {"tm": tm_peer(d)})

    leaving = mm(carry[...], tr[times - 1])
    ot_own[0] = leaving[:half]
    ot_own[1] = leaving[half:]
    for d in range(1, n_sp):
        peer = sp_peer(d)
        send(
            ot_own.at[lax.rem(peer, 2)], ot_rx.at[d - 1], (s_sem.at[OR], r_sem.at[OR]),
            {"space": peer},
        )

    reduce_cores(0)
    heads, tails = group_scans(tr, times // 4)
    for g in range(times // 4):
        for i in range(1, 4):
            scan_buf[g, i - 1] = heads[g][i]
        for i in range(1, 3):
            scan_buf[g, 2 + i] = tails[g][i]
    for k in range(1, own):
        reduce_cores(k)
    heads = [
        (tr[4 * g], scan_buf[g, 0], scan_buf[g, 1], scan_buf[g, 2]) for g in range(times // 4)
    ]
    tails = [
        (None, scan_buf[g, 3], scan_buf[g, 4], tr[4 * g + 3]) for g in range(times // 4)
    ]
    block_scans(heads, tails, pre_out, suf)

    wait(p_buf.at[c, pl.ds(0, n_tm - 1)], r_sem.at[PB])
    send(p_buf.at[c], p_buf.at[c], (s_sem.at[PF], r_sem.at[PF]), {"space": partner})

    wait(ot_rx, r_sem.at[OR])
    summed = ot_own[c]
    for d in range(1, n_sp):
        summed = summed + ot_rx[d - 1]
    ot_buf[c, me] = summed
    for d in range(1, n_tm):
        send(
            ot_buf.at[c, me], ot_buf.at[c, me], (s_sem.at[OT], r_sem.at[OT]), {"tm": tm_peer(d)}
        )

    wait(p_buf.at[c], r_sem.at[PF])

    rows = lax.broadcasted_iota(jnp.int32, (members, members), 0)
    cols = lax.broadcasted_iota(jnp.int32, (members, members), 1)
    identity = jnp.where(rows == cols, 1.0, 0.0).astype(f32)

    def block(b):
        return jnp.concatenate([p_buf[0, b], p_buf[1, b]], axis=0)

    later = jnp.where(n_tm - 1 > me, block(n_tm - 1), identity)
    for b in reversed(range(n_tm // 2, n_tm - 1)):
        later = mm(jnp.where(b > me, block(b), identity), later)
    prod_out[times] = later
    hand_round(0)
    later = prod_out[times]
    for b in reversed(range(1, n_tm // 2)):
        later = mm(jnp.where(b > me, block(b), identity), later)
    prod_out[times] = later
    for k in range(1, own):
        hand_round(k)
    later = prod_out[times]
    pre_out[0] = identity
    for b in range(n_tm - 1):
        p_out[b] = jnp.where(b < me, block(b), identity)
    for t in range(times):
        prod_out[t] = mm(suf[t], later)

    def big_products(first, last):
        for t in range(first, last):
            factor = prod_out[t].astype(bf16)
            sm_v[t] = lax.dot_general(
                factor, e_v[t], (((0,), (0,)), ((), ())), preferred_element_type=f32
            ).astype(bf16)
            eg_v[t] = jnp.dot(factor, c_v[t], preferred_element_type=f32).astype(bf16)

    big_products(0, times // 2)
    forward_totals(0)
    big_products(times // 2, 3 * times // 4)
    wait(ot_buf.at[c, pl.ds(0, n_tm - 1)], r_sem.at[OT])
    send(ot_buf.at[c], ot_buf.at[c], (s_sem.at[OF], r_sem.at[OF]), {"space": partner})
    for k in range(1, own):
        forward_totals(k)
    big_products(3 * times // 4, times)
    wait(ot_buf.at[c], r_sem.at[OF])
    for b in range(n_tm - 1):
        ot_out[b] = jnp.where(
            b < me, jnp.concatenate([ot_buf[0, b], ot_buf[1, b]], axis=0), 0.0
        )
    for k in range(own):
        wait(lt_fin.at[k, c], lf_r.at[k])
    for k in range(own):
        for q in range(n_y):
            for core in range(2):
                lt_out[2 * (k * n_y + q) + core] = lt_fin[k, core, q]
    wait(p_buf.at[c, pl.ds(0, n_tm - 1)], s_sem.at[PB])
    wait(p_buf.at[c], s_sem.at[PF])
    wait(ltp.at[c], s_sem.at[LP])
    wait(lt_ry, s_sem.at[LY])
    wait(lt_ry, s_sem.at[LA])
    wait(lt_fin.at[:, c], s_sem.at[LF])
    wait(ot_rx, s_sem.at[OR])
    wait(ot_buf.at[c, pl.ds(0, n_tm - 1)], s_sem.at[OT])
    wait(ot_buf.at[c], s_sem.at[OF])


def output_kernel(
    times, members, scale,
    sm_v, eg_v, lt, pre, prod, blocks, leaving,
    sm_hbm, eg_hbm, tg_hbm,
    tg, carry, sems, tg_sem,
):
    copies = []

    def write(q):
        part = pl.ds(q * (times // 4), times // 4)
        for k, (src, dst) in enumerate(((sm_v, sm_hbm), (eg_v, eg_hbm))):
            copy = pltpu.make_async_copy(src.at[part], dst.at[part], sems.at[k, q])
            copy.start()
            copies.append(copy)

    for q in range(4):
        write(q)
    last = blocks.shape[0]
    entering = leaving[0]
    for k, (first, stop) in enumerate(((1, last // 2), (last // 2, last))):
        for b in range(first, stop):
            entering = mm(entering, blocks[b]) + leaving[b]
        carry[...] = entering
        copies[k].wait()
        entering = carry[...]
    for q in range(2):
        part = pl.ds(q * (times // 2), times // 2)
        entering = carry[...]
        for t in range(q * (times // 2), (q + 1) * (times // 2)):
            total = unpack(lt[t], members) + mm(entering, pre[t])
            tg[t] = mm(prod[t + 1], total).T * scale
        copies[2 + q].wait()
        copy = pltpu.make_async_copy(tg.at[part], tg_hbm.at[part], tg_sem.at[q])
        copy.start()
        copies.append(copy)
    for copy in copies[4:]:
        copy.wait()


def shards(n_tm, n_sp, ensembles, cotangents, transforms):
    times, members, cells = ensembles.shape
    half = members // 2
    n_y = n_sp // 2
    per_core = times // 2
    own = per_core // n_y
    square = (members, members)
    halves = (half, members)
    packed = (half + members // 5, 128)
    anywhere = pl.BlockSpec(memory_space=pl.ANY)
    vmem = pl.BlockSpec(memory_space=pltpu.VMEM)
    dma = pltpu.SemaphoreType.DMA
    shape = jax.ShapeDtypeStruct
    big = shape((times, members, cells), bf16)
    stack = shape((times,) + square, f32)
    chain = shape((n_tm - 1,) + square, f32)
    passed = pl.pallas_call(
        functools.partial(exchange_kernel, n_tm, n_sp, times, members),
        out_shape=[
            big, big, shape((times,) + packed, f32), stack,
            shape((times + 1,) + square, f32), chain, chain,
        ],
        in_specs=[anywhere] * 3,
        out_specs=[vmem] * 7,
        scratch_shapes=[
            pltpu.VMEM((times, members, cells), bf16),
            pltpu.VMEM((times, members, cells), bf16),
            pltpu.VMEM((times,) + square, f32),
            pltpu.VMEM((2,) + halves, f32),
            pltpu.VMEM((2, n_tm) + halves, f32),
            pltpu.VMEM((2, per_core) + packed, f32),
            pltpu.VMEM((per_core,) + packed, f32),
            pltpu.VMEM((per_core,) + packed, f32),
            pltpu.VMEM((own, n_y - 1) + packed, f32),
            pltpu.VMEM((own, 2, n_y) + packed, f32),
            pltpu.VMEM((2,) + halves, f32),
            pltpu.VMEM((n_sp - 1,) + halves, f32),
            pltpu.VMEM((2, n_tm) + halves, f32),
            pltpu.VMEM((times,) + square, f32),
            pltpu.VMEM((times // 4, 5) + square, f32),
            pltpu.VMEM((times,) + square, f32),
            pltpu.VMEM(square, f32),
            dma((11,)),
            dma((9,)), dma((5,)), dma((own,)), dma((own,)), dma((own,)), dma((own,)),
        ],
        compiler_params=pltpu.CompilerParams(
            collective_id=0, has_side_effects=True, vmem_limit_bytes=34 * 2**20
        ),
        name="exchange",
    )(*(pltpu.with_memory_space_constraint(a, pltpu.HBM) for a in (ensembles, cotangents, transforms)))
    scale = 1.0 / math.sqrt(cells * n_sp * times * n_tm)
    return pl.pallas_call(
        functools.partial(output_kernel, times, members, scale),
        out_shape=[big, big, stack],
        in_specs=[vmem] * 7,
        out_specs=[anywhere] * 3,
        scratch_shapes=[
            pltpu.VMEM((times,) + square, f32), pltpu.VMEM(square, f32), dma((2, 4)), dma((2,)),
        ],
        compiler_params=pltpu.CompilerParams(vmem_limit_bytes=8 * 2**20),
        name="outputs",
    )(*passed)


def solution(mesh):
    specs = (P("tm", None, "space"), P("tm", None, "space"), P("tm", None, None))
    return jax.shard_map(
        functools.partial(shards, mesh.shape["tm"], mesh.shape["space"]),
        mesh=mesh,
        in_specs=specs,
        out_specs=specs,
        check_vma=False,
    )
```

```python
import functools
import math

import jax
import jax.numpy as jnp
from jax import lax
from jax.experimental import pallas as pl
from jax.experimental.pallas import tpu as pltpu
from jax.sharding import PartitionSpec as P

MESH = pl.DeviceIdType.MESH
PB, PF, OR, OT, OF, OC, LP, LY, LA, LF = range(10)
f32 = jnp.float32
bf16 = jnp.bfloat16


def mm(a, b, dims=((1,), (0,))):
    return lax.dot_general(
        a, b, (dims, ((), ())), precision=lax.Precision.HIGHEST, preferred_element_type=f32
    )


def group_scans(tr, g):
    w = [tr[4 * g + i] for i in range(4)]
    w01, w23 = mm(w[0], w[1]), mm(w[2], w[3])
    heads = (w[0], w01, mm(w01, w[2]), mm(w01, w23))
    tails = (None, mm(w[1], w23), w23, w[3])
    return heads, tails


def block_scans(heads, tails, prefix_ref, suffix_ref):
    groups = len(heads)
    before = None
    for g in range(groups):
        for i in range(4):
            if g == 0 and i == 0:
                continue
            if i == 0:
                prefix_ref[4 * g] = before
            elif g == 0:
                prefix_ref[i] = heads[0][i - 1]
            else:
                prefix_ref[4 * g + i] = mm(before, heads[g][i - 1])
        before = heads[g][3] if g == 0 else mm(before, heads[g][3])
    after = None
    for g in reversed(range(groups)):
        whole = heads[g][3]
        parts = (whole,) + tails[g][1:]
        for i in range(4):
            suffix_ref[4 * g + i] = parts[i] if after is None else mm(parts[i], after)
        after = whole if after is None else mm(whole, after)


def block_total(tr, count):
    level = [tr[i] for i in range(count)]
    while len(level) > 1:
        level = [mm(level[i], level[i + 1]) for i in range(0, len(level), 2)]
    return level[0]


def pack(square):
    rows = square.shape[0]
    left, rest, tall = 64, rows - 64, rows // 5
    wide = jnp.concatenate([square[: rows // 2, :left], square[rows // 2 :, :left]], axis=1)
    pieces = [square[tall * g : tall * (g + 1), left:] for g in range(5)]
    pieces.append(jnp.zeros((tall, 2 * left - 5 * rest), f32))
    return jnp.concatenate([wide, jnp.concatenate(pieces, axis=1)], axis=0)


def unpack(packed, rows):
    left, rest, tall = 64, rows - 64, rows // 5
    wide, tail = packed[: rows // 2], packed[rows // 2 :]
    first = jnp.concatenate([wide[:, :left], wide[:, left:]], axis=0)
    last = jnp.concatenate([tail[:, rest * g : rest * (g + 1)] for g in range(5)], axis=0)
    return jnp.concatenate([first, last], axis=1)


def exchange_kernel(
    n_tm, n_sp, times, members,
    e_hbm, c_hbm, t_hbm,
    sm_v, eg_v, lt_out, pre_out, prod_out, p_out, ot_out,
    e_v, c_v, tr, p_own, p_buf, ltp, lt_rx, lt_core, lt_ry, lt_fin, ot_own, ot_rx, ot_core, ot_buf, suf, scan_buf, gram, carry,
    in_sem, s_sem, r_sem, lp_r, ly_r, la_r, lf_r,
):
    half = members // 2
    n_y = n_sp // 2
    own = times // 2 // n_y
    batch = times // own
    me = lax.axis_index("tm")
    sp = lax.axis_index("space")
    y = sp // 2
    c = lax.rem(sp, 2)
    partner = 2 * y + (1 - c)

    def tm_peer(d):
        return lax.rem(me + d, n_tm)

    def sp_peer(d):
        return lax.rem(sp + d, n_sp)

    def send(src, dst, sems, device):
        pltpu.make_async_remote_copy(
            src_ref=src, dst_ref=dst, send_sem=sems[0], recv_sem=sems[1],
            device_id=device, device_id_type=MESH,
        ).start()

    def wait(ref, sem):
        pltpu.make_async_copy(ref, ref, sem).wait()

    t_copy = pltpu.make_async_copy(t_hbm, tr, in_sem.at[10])
    t_copy.start()
    groups = [(0, 4), (4, 8), (8, 12), (12, 14), (14, 16)]
    loads = []
    for g, (first, last) in enumerate(groups):
        part = pl.ds(first, last - first)
        loads.append((
            pltpu.make_async_copy(e_hbm.at[part], e_v.at[part], in_sem.at[2 * g]),
            pltpu.make_async_copy(c_hbm.at[part], c_v.at[part], in_sem.at[2 * g + 1]),
        ))
        for copy in loads[-1]:
            copy.start()

    barrier = pltpu.get_barrier_semaphore()
    for d in range(1, n_tm):
        pl.semaphore_signal(barrier, inc=1, device_id={"tm": tm_peer(d)}, device_id_type=MESH)
    for d in range(1, n_sp):
        pl.semaphore_signal(barrier, inc=1, device_id={"space": sp_peer(d)}, device_id_type=MESH)

    t_copy.wait()
    total = block_total(tr, times)
    p_own[0] = total[:half]
    p_own[1] = total[half:]
    p_buf[c, me] = p_own[c]

    def send_pairs(first, last):
        k = first // n_y
        part = pl.ds(first, last - first)
        send(ltp.at[1 - c, part], lt_rx.at[part], (s_sem.at[LP], lp_r.at[k]), {"space": partner})

    def reduce_cores(k):
        wait(lt_rx.at[pl.ds(k * n_y, n_y)], lp_r.at[k])
        for j in range(k * n_y, (k + 1) * n_y):
            lt_core[j] = ltp[c, j] + lt_rx[j]
        for d in range(1, n_y):
            q = lax.rem(y + d, n_y)
            send(
                lt_core.at[k * n_y + q], lt_ry.at[k, d - 1], (s_sem.at[LY], ly_r.at[k]),
                {"space": 2 * q + c},
            )

    def hand_round(k):
        wait(lt_ry.at[k], ly_r.at[k])
        mine = lt_core[k * n_y + y]
        for d in range(1, n_y):
            mine = mine + lt_ry[k, d - 1]
        lt_fin[k, c, y] = mine
        for d in range(1, n_y):
            q = lax.rem(y + d, n_y)
            send(
                lt_fin.at[k, c, y], lt_fin.at[k, c, y], (s_sem.at[LA], la_r.at[k]),
                {"space": 2 * q + c},
            )

    def forward_totals(k):
        wait(lt_ry.at[k], la_r.at[k])
        send(lt_fin.at[k, c], lt_fin.at[k, c], (s_sem.at[LF], lf_r.at[k]), {"space": partner})

    before = (0, 0)
    for g, (first, last) in enumerate(groups + [(times, times)]):
        if last > first:
            for copy in loads[g]:
                copy.wait()
        if before[0]:
            state = carry[...]
        for k in range(max(last - first, before[1] - before[0])):
            if first + k < last:
                t = first + k
                gram[t] = lax.dot_general(
                    c_v[t], e_v[t], (((1,), (1,)), ((), ())), preferred_element_type=f32
                )
            if before[0] + k < before[1]:
                t = before[0] + k
                state = gram[t] if t == 0 else gram[t] + mm(state, tr[t - 1])
                ltp[t % 2, t // 2] = pack(state)
        if before[1]:
            carry[...] = state
        if before[1]:
            send_pairs(before[0] // 2, before[1] // 2)
        before = (first, last)
        if g == 0:
            pl.semaphore_wait(barrier, n_tm - 1 + n_sp - 1)
            for d in range(1, n_tm):
                send(p_own.at[c], p_buf.at[c, me], (s_sem.at[PB], r_sem.at[PB]), {"tm": tm_peer(d)})

    leaving = mm(carry[...], tr[times - 1])
    ot_own[0] = leaving[:half]
    ot_own[1] = leaving[half:]
    send(ot_own.at[1 - c], ot_rx.at[n_y - 1], (s_sem.at[OC], r_sem.at[OC]), {"space": partner})

    def scan_groups(first, last):
        for g in range(first, last):
            heads, tails = group_scans(tr, g)
            for i in range(1, 4):
                scan_buf[g, i - 1] = heads[i]
            for i in range(1, 3):
                scan_buf[g, 2 + i] = tails[i]

    scan_groups(0, times // 8)
    wait(ot_own.at[0], r_sem.at[OC])
    ot_core[...] = ot_own[c] + ot_rx[n_y - 1]
    for d in range(1, n_y):
        q = lax.rem(y + d, n_y)
        send(ot_core, ot_rx.at[d - 1], (s_sem.at[OR], r_sem.at[OR]), {"space": 2 * q + c})
    reduce_cores(0)
    scan_groups(times // 8, times // 4)
    for k in range(1, own):
        reduce_cores(k)
    heads = [
        (tr[4 * g], scan_buf[g, 0], scan_buf[g, 1], scan_buf[g, 2]) for g in range(times // 4)
    ]
    tails = [
        (None, scan_buf[g, 3], scan_buf[g, 4], tr[4 * g + 3]) for g in range(times // 4)
    ]
    block_scans(heads, tails, pre_out, suf)

    wait(p_buf.at[c, pl.ds(0, n_tm - 1)], r_sem.at[PB])
    send(p_buf.at[c], p_buf.at[c], (s_sem.at[PF], r_sem.at[PF]), {"space": partner})

    wait(ot_rx.at[pl.ds(0, n_y - 1)], r_sem.at[OR])
    summed = ot_core[...]
    for d in range(1, n_y):
        summed = summed + ot_rx[d - 1]
    ot_buf[c, me] = summed
    for d in range(1, n_tm):
        send(
            ot_buf.at[c, me], ot_buf.at[c, me], (s_sem.at[OT], r_sem.at[OT]), {"tm": tm_peer(d)}
        )

    wait(p_buf.at[c], r_sem.at[PF])

    rows = lax.broadcasted_iota(jnp.int32, (members, members), 0)
    cols = lax.broadcasted_iota(jnp.int32, (members, members), 1)
    identity = jnp.where(rows == cols, 1.0, 0.0).astype(f32)

    def block(b):
        return jnp.concatenate([p_buf[0, b], p_buf[1, b]], axis=0)

    later = jnp.where(n_tm - 1 > me, block(n_tm - 1), identity)
    for b in reversed(range(n_tm // 2, n_tm - 1)):
        later = mm(jnp.where(b > me, block(b), identity), later)
    prod_out[times] = later
    hand_round(0)
    later = prod_out[times]
    for b in reversed(range(1, n_tm // 2)):
        later = mm(jnp.where(b > me, block(b), identity), later)
    prod_out[times] = later
    for k in range(1, own):
        hand_round(k)
    later = prod_out[times]
    pre_out[0] = identity
    for b in range(n_tm - 1):
        p_out[b] = jnp.where(b < me, block(b), identity)
    for t in range(times):
        prod_out[t] = mm(suf[t], later)

    def big_products(first, last):
        for t in range(first, last):
            factor = prod_out[t].astype(bf16)
            sm_v[t] = lax.dot_general(
                factor, e_v[t], (((0,), (0,)), ((), ())), preferred_element_type=f32
            ).astype(bf16)
            eg_v[t] = jnp.dot(factor, c_v[t], preferred_element_type=f32).astype(bf16)

    big_products(0, times // 2)
    forward_totals(0)
    big_products(times // 2, 3 * times // 4)
    wait(ot_buf.at[c, pl.ds(0, n_tm - 1)], r_sem.at[OT])
    send(ot_buf.at[c], ot_buf.at[c], (s_sem.at[OF], r_sem.at[OF]), {"space": partner})
    for k in range(1, own):
        forward_totals(k)
    big_products(3 * times // 4, times)
    for k in range(own):
        wait(lt_fin.at[k, c], lf_r.at[k])
    for k in range(own):
        for q in range(n_y):
            for core in range(2):
                lt_out[2 * (k * n_y + q) + core] = lt_fin[k, core, q]
    wait(ot_buf.at[c], r_sem.at[OF])
    for b in range(n_tm - 1):
        ot_out[b] = jnp.where(
            b < me, jnp.concatenate([ot_buf[0, b], ot_buf[1, b]], axis=0), 0.0
        )
    wait(p_buf.at[c, pl.ds(0, n_tm - 1)], s_sem.at[PB])
    wait(p_buf.at[c], s_sem.at[PF])
    wait(ltp.at[c], s_sem.at[LP])
    wait(lt_ry, s_sem.at[LY])
    wait(lt_ry, s_sem.at[LA])
    wait(lt_fin.at[:, c], s_sem.at[LF])
    wait(ot_rx.at[pl.ds(0, n_y - 1)], s_sem.at[OR])
    wait(ot_own.at[0], s_sem.at[OC])
    wait(ot_buf.at[c, pl.ds(0, n_tm - 1)], s_sem.at[OT])
    wait(ot_buf.at[c], s_sem.at[OF])


def output_kernel(
    times, members, scale,
    sm_v, eg_v, lt, pre, prod, blocks, leaving,
    sm_hbm, eg_hbm, tg_hbm,
    tg, carry, sems, tg_sem,
):
    copies = []

    def write(q):
        part = pl.ds(q * (times // 4), times // 4)
        for k, (src, dst) in enumerate(((sm_v, sm_hbm), (eg_v, eg_hbm))):
            copy = pltpu.make_async_copy(src.at[part], dst.at[part], sems.at[k, q])
            copy.start()
            copies.append(copy)

    for q in range(4):
        write(q)
    last = blocks.shape[0]
    entering = leaving[0]
    tg[0] = unpack(lt[0], members)
    for t in range(last, times):
        tg[t] = unpack(lt[t], members)
    for k, (first, stop) in enumerate(((1, last // 2), (last // 2, last))):
        for b in range(first, stop):
            entering = mm(entering, blocks[b]) + leaving[b]
            tg[b] = unpack(lt[b], members)
        carry[...] = entering
        copies[k].wait()
        entering = carry[...]
    for q in range(2):
        part = pl.ds(q * (times // 2), times // 2)
        entering = carry[...]
        for t in range(q * (times // 2), (q + 1) * (times // 2)):
            total = tg[t] + mm(entering, pre[t])
            tg[t] = mm(prod[t + 1], total).T * scale
        copies[2 + q].wait()
        copy = pltpu.make_async_copy(tg.at[part], tg_hbm.at[part], tg_sem.at[q])
        copy.start()
        copies.append(copy)
    for copy in copies[4:]:
        copy.wait()


def shards(n_tm, n_sp, ensembles, cotangents, transforms):
    times, members, cells = ensembles.shape
    half = members // 2
    n_y = n_sp // 2
    per_core = times // 2
    own = per_core // n_y
    square = (members, members)
    halves = (half, members)
    packed = (half + members // 5, 128)
    anywhere = pl.BlockSpec(memory_space=pl.ANY)
    vmem = pl.BlockSpec(memory_space=pltpu.VMEM)
    dma = pltpu.SemaphoreType.DMA
    shape = jax.ShapeDtypeStruct
    big = shape((times, members, cells), bf16)
    stack = shape((times,) + square, f32)
    chain = shape((n_tm - 1,) + square, f32)
    passed = pl.pallas_call(
        functools.partial(exchange_kernel, n_tm, n_sp, times, members),
        out_shape=[
            big, big, shape((times,) + packed, f32), stack,
            shape((times + 1,) + square, f32), chain, chain,
        ],
        in_specs=[anywhere] * 3,
        out_specs=[vmem] * 7,
        scratch_shapes=[
            pltpu.VMEM((times, members, cells), bf16),
            pltpu.VMEM((times, members, cells), bf16),
            pltpu.VMEM((times,) + square, f32),
            pltpu.VMEM((2,) + halves, f32),
            pltpu.VMEM((2, n_tm) + halves, f32),
            pltpu.VMEM((2, per_core) + packed, f32),
            pltpu.VMEM((per_core,) + packed, f32),
            pltpu.VMEM((per_core,) + packed, f32),
            pltpu.VMEM((own, n_y - 1) + packed, f32),
            pltpu.VMEM((own, 2, n_y) + packed, f32),
            pltpu.VMEM((2,) + halves, f32),
            pltpu.VMEM((n_y,) + halves, f32),
            pltpu.VMEM(halves, f32),
            pltpu.VMEM((2, n_tm) + halves, f32),
            pltpu.VMEM((times,) + square, f32),
            pltpu.VMEM((times // 4, 5) + square, f32),
            pltpu.VMEM((times,) + square, f32),
            pltpu.VMEM(square, f32),
            dma((11,)),
            dma((10,)), dma((6,)), dma((own,)), dma((own,)), dma((own,)), dma((own,)),
        ],
        compiler_params=pltpu.CompilerParams(
            collective_id=0, has_side_effects=True, vmem_limit_bytes=34 * 2**20
        ),
        name="exchange",
    )(*(pltpu.with_memory_space_constraint(a, pltpu.HBM) for a in (ensembles, cotangents, transforms)))
    scale = 1.0 / math.sqrt(cells * n_sp * times * n_tm)
    return pl.pallas_call(
        functools.partial(output_kernel, times, members, scale),
        out_shape=[big, big, stack],
        in_specs=[vmem] * 7,
        out_specs=[anywhere] * 3,
        scratch_shapes=[
            pltpu.VMEM((times,) + square, f32), pltpu.VMEM(square, f32), dma((2, 4)), dma((2,)),
        ],
        compiler_params=pltpu.CompilerParams(vmem_limit_bytes=8 * 2**20),
        name="outputs",
    )(*passed)


def solution(mesh):
    specs = (P("tm", None, "space"), P("tm", None, "space"), P("tm", None, None))
    return jax.shard_map(
        functools.partial(shards, mesh.shape["tm"], mesh.shape["space"]),
        mesh=mesh,
        in_specs=specs,
        out_specs=specs,
        check_vma=False,
    )
```
